128 devices in a mesh: vir: 8 (over y_hi, x), occ: 16 (over y_lo, z, core).
Axes of the slice: x: 4, y: 4 (y_hi: 2, y_lo: 2; y = y_hi * 2 + y_lo), z: 4, core: 2. Of those that a mesh axis runs over, the one named last changes fastest.
Arguments:
- amplitudes: bfloat16 [4096, 8192], P('occ', 'vir'), may hold values from -6 to 6
- ladder_integrals: bfloat16 [8192, 8192], P('occ', 'vir'), may hold values from -0.0625 to 0.0625
- crossed_integrals: bfloat16 [2, 4096, 4096], P(None, 'occ', 'vir'), may hold values from -0.09375 to 0.09375
- vir_counts: int32 [8], replicated, may hold values from 1 to 64, 480 in all
Outputs:
- residual: bfloat16 [4096, 8192], P('occ', 'vir')
The draws below stay inside these ranges and needn't reach their ends.
Inputs may be any that keep to these rules, and one draw needn't show every extreme that they name: `vir_counts`: the counts of all 8 irreps sum to 480 and the largest is exactly 64.
All inputs are finite; a program needn't handle non-finite values.
Results may differ from the reference program's by a relative error of at most 0.004.
Values may be sent and summed in bfloat16 or wider, within the bound.
A program may use at most 128 MiB of HBM per device.

```python
import math
import jax
import jax.numpy as jnp
import numpy as np

O = 64
VS = 64
NB = 2
IRREPS = 8
OP = 4096
BP = 4096
VP = 8192
OV = 4096


def steps_of(own_key, extent, shards, smallest, largest):
    def one(position, shards_of):
        heights = jax.random.uniform(jax.random.fold_in(jax.random.fold_in(own_key, 6), position), (shards_of,), jnp.float32, smallest / len(shards), largest / len(shards))
        return jnp.repeat(jnp.exp(heights), extent[position] // shards_of).reshape((-1,) + (1,) * (len(extent) - position - 1))

    level = one(*shards[0])
    for cut in shards[1:]:
        level = level * one(*cut)
    return level


def length_profile(amount, total, most, skew):
    weights = [(1 << 20) // math.isqrt(grade ** skew) + 1 for grade in range(2, amount + 1)]
    rest, given = total - most - (amount - 1), [1] * (amount - 1)
    while rest > 0:
        free = [i for i in range(amount - 1) if given[i] < most]
        whole, remaining = sum([weights[i] for i in free]), rest
        for i in free:
            extra = min(most - given[i], max(1, remaining * weights[i] // whole), rest)
            given[i] = given[i] + extra
            rest = rest - extra
    return np.array([most] + given)


def ragged_sizes(own_key, number_of, total, reach, lean):
    if number_of == 2:
        one = jax.random.randint(own_key, (), max(1, total - reach), min(reach, total - 1) + 1)
        return jnp.stack([one, total - one])
    tallies = jnp.asarray(length_profile(number_of, total, reach, lean), jnp.int32)
    twos = (number_of - 1) // 2
    donor, sink = tallies[1:1 + 2 * twos:2], tallies[2:2 + 2 * twos:2]
    slack = jnp.minimum(donor - 1, reach - sink)
    passed = jax.random.randint(jax.random.fold_in(own_key, 1), (twos,), 0, 1 << 20) % (slack + 1)
    tallies = tallies.at[1:1 + 2 * twos:2].set(donor - passed).at[2:2 + 2 * twos:2].set(sink + passed)
    return tallies[jax.random.permutation(jax.random.fold_in(own_key, 2), number_of)]


def noise(rng, extent, deviation, most, split=(), kind=jnp.bfloat16):
    gain = steps_of(rng, extent, split, -0.22, 0.18) if split else 1.0
    result = jax.random.normal(rng, extent, jnp.float32) * deviation * gain
    return jnp.minimum(jnp.maximum(result, -most), most).astype(kind)


def setup_inputs(seed: int = 0) -> dict:
    streams_of = jax.random.split(jax.random.key(seed), 5)
    amplitudes = noise(streams_of[0], (OP, VP), 1.0, 6.0, ((0, 16), (1, 8)))
    ladder_integrals = noise(streams_of[1], (VP, VP), VP ** -0.5, 0.0625, ((0, 16), (1, 8)))
    crossed_integrals = noise(streams_of[2], (NB, OV, OV), OV ** -0.5, 0.09375, ((1, 16), (2, 8)))
    vir_counts = ragged_sizes(streams_of[3], IRREPS, IRREPS * VS * 15 // 16, VS, 1).astype(jnp.int32)
    return dict(amplitudes=amplitudes, ladder_integrals=ladder_integrals, crossed_integrals=crossed_integrals, vir_counts=vir_counts)


def build_mask(vir_counts):
    slot_index = jnp.arange(VS, dtype=jnp.int32)
    blocks = []
    for block_index in range(NB):
        first_act = (slot_index < vir_counts[2 * block_index]).astype(jnp.float32)
        second_act = (slot_index < vir_counts[2 * block_index + 1]).astype(jnp.float32)
        blocks.append((first_act[:, None] * second_act[None, :]).reshape(BP))
    return jnp.concatenate(blocks)


def reference(amplitudes, ladder_integrals, crossed_integrals, vir_counts):
    pair_mask = build_mask(vir_counts)
    masked = amplitudes * pair_mask.astype(amplitudes.dtype)[None, :]
    ladder = jnp.dot(masked.astype(jnp.float32), ladder_integrals.astype(jnp.float32), preferred_element_type=jnp.float32)
    reordered = masked.reshape(O, O, NB, VS, VS).transpose(2, 0, 3, 1, 4).reshape(NB, O * VS, O * VS)
    crossed_sum = jnp.einsum("gxy,gyz->gxz", reordered.astype(jnp.float32), crossed_integrals.astype(jnp.float32))
    crossed_term = crossed_sum.astype(jnp.bfloat16)
    returned = crossed_term.reshape(NB, O, VS, O, VS).transpose(1, 3, 0, 2, 4).reshape(O * O, NB * BP)
    total = (ladder + returned.astype(jnp.float32)) * pair_mask[None, :]
    return total.astype(jnp.bfloat16)
```

```python
import jax
import jax.numpy as jnp
from jax import lax
from jax.experimental import pallas as pl
from jax.experimental.pallas import tpu as pltpu
from jax.sharding import PartitionSpec as P

MESH = pl.DeviceIdType.MESH
F32 = jnp.float32
BF16 = jnp.bfloat16


def both(*conds):
    out = conds[0]
    for other in conds[1:]:
        out = jnp.logical_and(out, other)
    return out


def device(yh, x, yl, z, c):
    return (yh * 4 + x, (yl * 4 + z) * 2 + c)


def kernel(
    cnt, amp, lad, xin, out,
    mb, lb, xb, mm, rr, ff, acc, dd, pf, cs, cr, xs, xr,
    s_l, s_lf, s_m, s_mx, s_mf, s_xa, s_xd, s_xz, s_xf, s_c, s_o,
    r_m, r_l, r_x, r_c, r_o,
):
    v = lax.axis_index("vir")
    o = lax.axis_index("occ")
    yh = lax.div(v, 4)
    x = lax.rem(v, 4)
    yl = lax.div(o, 8)
    z = lax.rem(lax.div(o, 2), 4)
    c = lax.rem(o, 2)
    xp, xm = lax.rem(x + 1, 4), lax.rem(x + 3, 4)
    zp, zm, zo = lax.rem(z + 1, 4), lax.rem(z + 3, 4), lax.rem(z + 2, 4)
    q = yl * 2 + c

    def remote(src, dst, ss, rs, target):
        return pltpu.make_async_remote_copy(
            src_ref=src, dst_ref=dst, send_sem=ss, recv_sem=rs, device_id=target, device_id_type=MESH
        )

    sent = []

    def put(src, dst, ss, rs, target, cond=None, is_self=None):
        def go():
            remote(src, dst, ss, rs, target).start()

        def fin():
            remote(src, dst, ss, rs, target).wait_send()

        conds = [] if cond is None else [cond]
        if is_self is not None:
            conds.append(jnp.logical_not(is_self))

            @pl.when(both(*([] if cond is None else [cond]), is_self))
            def _():
                pltpu.make_async_copy(src, dst, rs).start()

        if conds:
            pl.when(both(*conds))(go)
            sent.append((both(*conds), fin))
        else:
            go()
            sent.append((None, fin))

    def arrived(dst, rs):
        pltpu.make_async_copy(dst, dst, rs).wait()

    def mslot(u, k):
        return mb.at[u, pl.ds(pl.multiple_of(k * 256, 256), 256)]

    def lslot(t, hf):
        return lb.at[pl.ds(pl.multiple_of((t * 2 + hf) * 256, 256), 256)]

    def xslot(k):
        return xb.at[pl.ds(pl.multiple_of(k * 256, 256), 256)]

    barrier = pltpu.get_barrier_semaphore()
    for dv in range(8):
        for dq in range(4):
            if dv == 0 and dq == 0:
                continue
            tv = lax.rem(v + dv, 8)
            tq = lax.rem(q + dq, 4)
            to = (lax.div(tq, 2) * 4 + z) * 2 + lax.rem(tq, 2)
            pl.semaphore_signal(barrier, inc=1, device_id=(tv, to), device_id_type=MESH)
    for tz in (zp, zm):
        for tc in range(2):
            pl.semaphore_signal(barrier, inc=1, device_id=device(yh, x, yl, tz, tc), device_id_type=MESH)
    pl.semaphore_wait(barrier, 35)

    ls = lax.div(z, 2)
    lt = 2 * lax.rem(z, 2) + c
    for hf, d in ((0, 0), (1, 1), (1, 0), (0, 1)):
        put(lad.at[pl.ds(hf * 256, 256)], lslot(lt, hf), s_l.at[d, hf], r_l.at[lt, hf],
            device(yh, x, yl, (zp, zm)[d], ls))
    ms = lax.div(x, 2)
    mu = lax.rem(x, 2)
    for t in range(2):
        put(amp, mslot(mu, q), s_m.at[t], r_m.at[mu, q], device(t, x, yh, z, ms),
            is_self=both(yh == t, yl == yh, c == ms))
    for hf in range(2):
        put(lad.at[pl.ds(hf * 256, 256)], lslot(lt, hf), s_l.at[2, hf], r_l.at[lt, hf],
            device(yh, x, yl, z, ls), is_self=c == ls)
    put(xin.at[1 - yl], xslot(o), s_xa, r_x.at[o], device(yh, x, 1 - yl, z, c))
    pltpu.make_async_copy(xin.at[yl], xslot(o), r_x.at[o]).start()
    put(xin.at[yl], xslot(o), s_xd.at[0], r_x.at[o], device(yh, x, yl, z, 1 - c))

    origin = c == ms
    for k in range(4):
        @pl.when(origin)
        def _():
            arrived(mslot(mu, k), r_m.at[mu, k])

        for d in range(2):
            put(mslot(mu, k), mslot(mu, k), s_mx.at[k, d], r_m.at[mu, k],
                device(yh, (xp, xm)[d], yl, z, c), cond=origin)

    for u in range(2):
        dist = lax.rem(z - (2 * c + u) + 4, 4)
        for d in range(2):
            passing = dist == (1, 3)[d]
            for tc in range(2):
                t = 2 * u + tc

                @pl.when(passing)
                def _():
                    arrived(lslot(t, d), r_l.at[t, d])

                put(lslot(t, d), lslot(t, d), s_lf.at[t, d], r_l.at[t, d],
                    device(yh, x, yl, (zp, zm)[d], c), cond=passing)

    for d in range(2):
        put(xin.at[yl], xslot(o), s_xz.at[0, d], r_x.at[o], device(yh, x, yl, (zp, zm)[d], c))
    op = ((1 - yl) * 4 + z) * 2 + c
    arrived(xslot(op), r_x.at[op])
    put(xslot(op), xslot(op), s_xd.at[1], r_x.at[op], device(yh, x, yl, z, 1 - c))
    for d in range(2):
        put(xslot(op), xslot(op), s_xz.at[1, d], r_x.at[op], device(yh, x, yl, (zp, zm)[d], c))

    for u in range(2):
        dist = lax.rem(x - (2 * c + u) + 4, 4)
        for d in range(2):
            passing = dist == (1, 3)[d]
            for k in (d, 2 + d):
                @pl.when(passing)
                def _():
                    arrived(mslot(u, k), r_m.at[u, k])

                put(mslot(u, k), mslot(u, k), s_mf.at[u, k], r_m.at[u, k],
                    device(yh, (xp, xm)[d], yl, z, c), cond=passing)

    for d in range(2):
        for b in range(2):
            k = (b * 4 + (zm, zp)[d]) * 2 + c
            arrived(xslot(k), r_x.at[k])
            if b == d:
                put(xslot(k), xslot(k), s_xf.at[d], r_x.at[k], device(yh, x, yl, (zp, zm)[d], c))
            put(xslot(k), xslot(k), s_xd.at[2 + d * 2 + b], r_x.at[k], device(yh, x, yl, z, 1 - c))
    for b in range(2):
        k = (b * 4 + zo) * 2 + c
        arrived(xslot(k), r_x.at[k])
        put(xslot(k), xslot(k), s_xd.at[6 + b], r_x.at[k], device(yh, x, yl, z, 1 - c))

    for u in range(2):
        dist = lax.rem(x - (2 * c + u) + 4, 4)
        for k in range(4):
            d = k % 2

            @pl.when(jnp.logical_and(dist != 0, dist != (1, 3)[d]))
            def _():
                arrived(mslot(u, k), r_m.at[u, k])
    for u in range(2):
        dist = lax.rem(z - (2 * c + u) + 4, 4)
        for hf in range(2):
            for tc in range(2):
                t = 2 * u + tc

                @pl.when(dist != (1, 3)[hf])
                def _():
                    arrived(lslot(t, hf), r_l.at[t, hf])

    lane = lax.broadcasted_iota(jnp.int32, (1, 1024), 1)
    slot_a = lax.div(lane, 64)
    slot_b = lax.rem(lane, 64)
    in_b = slot_b < cnt[2 * yl + 1]
    for u in range(2):
        in_a = slot_a + (32 * c + 16 * u) < cnt[2 * yl]
        mask = jnp.where(jnp.logical_and(in_a, in_b), 1.0, 0.0).astype(BF16)

        @pl.loop(0, 32)
        def _(r):
            rows = pl.ds(pl.multiple_of(r * 32, 32), 32)
            mm[rows, u * 1024:(u + 1) * 1024] = mb[u, rows, :] * mask

    for rel in (2, 1, 3, 0):
        tq = lax.rem(q + rel, 4)

        @pl.loop(0, 4)
        def _(n):
            rows = pl.ds(pl.multiple_of(tq * 256, 256), 256)
            cols = pl.ds(pl.multiple_of(n * 256, 256), 256)
            part = jnp.dot(mm[rows, :], lb[:, cols], preferred_element_type=F32)
            if rel:
                cs[rel - 1, :, cols] = part.astype(BF16)
            else:
                pf[:, cols] = part

        if rel:
            put(cs.at[rel - 1], cr.at[rel - 1], s_c.at[rel - 1], r_c.at[rel - 1],
                device(yh, x, lax.div(tq, 2), z, lax.rem(tq, 2)))

    low = lax.broadcasted_iota(jnp.int32, (16, 128), 1) < 64

    @pl.loop(0, 16)
    def _(ap):
        cols = pl.ds(pl.multiple_of(ap * 128, 128), 128)

        @pl.loop(0, 16)
        def _(r):
            rows = pl.ds(pl.multiple_of(r * 64, 64), 64)
            ff[rows, :] = mm[rows, cols].astype(F32)

        for kp in range(32):
            v0 = ff[pl.ds(2 * kp, 16, stride=64), :]
            v1 = ff[pl.ds(2 * kp + 1, 16, stride=64), :]
            turned = pltpu.roll(jnp.where(low, v1, v0), 64, 1)
            even = jnp.where(low, v0, turned)
            odd = jnp.where(low, turned, v1)
            row = pl.multiple_of(ap * 32, 32)
            rr[pl.ds(row, 32), kp * 128:(kp + 1) * 128] = jnp.concatenate([even, odd], axis=0).astype(BF16)

    arrived(xslot(o), r_x.at[o])
    for b in range(2):
        for tz in range(4):
            k = (b * 4 + tz) * 2 + 1 - c
            arrived(xslot(k), r_x.at[k])

    @pl.loop(0, 2)
    def _(m):
        for n in range(2):
            rows = pl.ds(pl.multiple_of(m * 256, 256), 256)
            acc[rows, n * 256:(n + 1) * 256] = jnp.dot(
                rr[rows, :], xb[:, n * 256:(n + 1) * 256], preferred_element_type=F32
            )

    low8 = lax.broadcasted_iota(jnp.int32, (8, 128), 1) < 64

    @pl.loop(0, 16)
    def _(ap):
        for jp in range(4):
            cols = slice(jp * 128, (jp + 1) * 128)
            for ih in range(2):
                v0 = acc[pl.ds(pl.multiple_of(ap * 32 + ih * 8, 8), 8), cols]
                v1 = acc[pl.ds(pl.multiple_of(ap * 32 + 16 + ih * 8, 8), 8), cols]
                turned = pltpu.roll(jnp.where(low8, v1, v0), 64, 1)
                dd[ap, pl.ds(ih * 64 + 2 * jp, 8, stride=8), :] = jnp.where(low8, v0, turned)
                dd[ap, pl.ds(ih * 64 + 2 * jp + 1, 8, stride=8), :] = jnp.where(low8, turned, v1)

    for u in range(2):
        for k in range(4):
            for ap in range(8):
                xs[u * 4 + k, :, ap * 128:(ap + 1) * 128] = dd[u * 8 + ap, k * 32:(k + 1) * 32, :].astype(BF16)
            put(xs.at[u * 4 + k], xr.at[v], s_o.at[u * 4 + k], r_o.at[v],
                device(yl, 2 * c + u, k // 2, z, k % 2),
                is_self=both(yh == yl, x == 2 * c + u, yl == k // 2, c == k % 2))

    for rel in range(3):
        arrived(cr.at[rel], r_c.at[rel])

    @pl.loop(0, 8)
    def _(r):
        rows = pl.ds(pl.multiple_of(r * 32, 32), 32)
        pf[rows, :] = (pf[rows, :] + cr[0, rows, :].astype(F32)) + (
            cr[1, rows, :].astype(F32) + cr[2, rows, :].astype(F32)
        )

    in_out = jnp.logical_and(slot_a + 16 * x < cnt[2 * yh], slot_b < cnt[2 * yh + 1])
    mask_out = jnp.where(in_out, 1.0, 0.0).astype(F32)
    for k in range(8):
        arrived(xr.at[k], r_o.at[k])
        got = xr[k].astype(F32)
        for i in range(4):
            rows = slice(i * 64 + k * 8, i * 64 + k * 8 + 8)
            pf[rows, :] = (pf[rows, :] + got[i * 8:(i + 1) * 8]) * mask_out

    @pl.loop(0, 8)
    def _(r):
        rows = pl.ds(pl.multiple_of(r * 32, 32), 32)
        out[rows, :] = pf[rows, :].astype(BF16)

    for cond, fin in sent:
        if cond is None:
            fin()
        else:
            pl.when(cond)(fin)


def per_device(amplitudes, ladder_integrals, crossed_integrals, vir_counts):
    dma = pltpu.SemaphoreType.DMA
    hbm = pl.BlockSpec(memory_space=pl.ANY)
    return pl.pallas_call(
        kernel,
        out_shape=jax.ShapeDtypeStruct((256, 1024), BF16),
        in_specs=[pl.BlockSpec(memory_space=pltpu.SMEM), hbm, hbm, hbm],
        out_specs=pl.BlockSpec(memory_space=pltpu.VMEM),
        scratch_shapes=[
            pltpu.VMEM((2, 1024, 1024), BF16),
            pltpu.VMEM((2048, 1024), BF16),
            pltpu.VMEM((4096, 512), BF16),
            pltpu.VMEM((1024, 2048), BF16),
            pltpu.VMEM((512, 4096), BF16),
            pltpu.VMEM((1024, 128), F32),
            pltpu.VMEM((512, 512), F32),
            pltpu.VMEM((16, 128, 128), F32),
            pltpu.VMEM((256, 1024), F32),
            pltpu.VMEM((3, 256, 1024), BF16),
            pltpu.VMEM((3, 256, 1024), BF16),
            pltpu.VMEM((8, 32, 1024), BF16),
            pltpu.VMEM((8, 32, 1024), BF16),
            dma((3, 2)), dma((4, 2)), dma((2,)), dma((4, 2)), dma((2, 4)),
            dma, dma((8,)), dma((2, 2)), dma((2,)), dma((3,)), dma((8,)),
            dma((2, 4)), dma((4, 2)), dma((16,)), dma((3,)), dma((8,)),
        ],
        compiler_params=pltpu.CompilerParams(
            collective_id=0, has_side_effects=True, vmem_limit_bytes=56 * 1024 * 1024
        ),
        name="residual",
    )(vir_counts, amplitudes, ladder_integrals, crossed_integrals)


def solution(mesh):
    in_specs = (P("occ", "vir"), P("occ", "vir"), P(None, "occ", "vir"), P())
    return jax.shard_map(
        per_device, mesh=mesh, in_specs=in_specs, out_specs=P("occ", "vir"), check_vma=False
    )
```

```python
import jax
import jax.numpy as jnp
from jax import lax
from jax.experimental import pallas as pl
from jax.experimental.pallas import tpu as pltpu
from jax.sharding import PartitionSpec as P

MESH = pl.DeviceIdType.MESH
F32 = jnp.float32
BF16 = jnp.bfloat16


def both(*conds):
    out = conds[0]
    for other in conds[1:]:
        out = jnp.logical_and(out, other)
    return out


def device(yh, x, yl, z, c):
    return (yh * 4 + x, (yl * 4 + z) * 2 + c)


def rows_of(k, size):
    return pl.ds(pl.multiple_of(k * size, size), size)


def kernel(
    cnt, amp, lad, xin, out,
    mb, lb, xb, tb, mm, pp, rr, ff, acc, dd, cs, cr, xs, xr,
    s_l, s_lf, s_m, s_mt, s_mx, s_mf, s_xa, s_xd, s_xz, s_xf, s_c, s_o,
    r_m, r_t, r_l, r_x, r_c, r_o,
):
    v = lax.axis_index("vir")
    o = lax.axis_index("occ")
    yh = lax.div(v, 4)
    x = lax.rem(v, 4)
    yl = lax.div(o, 8)
    z = lax.rem(lax.div(o, 2), 4)
    c = lax.rem(o, 2)
    xn = (lax.rem(x + 1, 4), lax.rem(x + 3, 4))
    zn = (lax.rem(z + 1, 4), lax.rem(z + 3, 4))
    zo = lax.rem(z + 2, 4)
    q = yl * 2 + c
    edge = yh == yl

    def remote(src, dst, ss, rs, target):
        return pltpu.make_async_remote_copy(
            src_ref=src, dst_ref=dst, send_sem=ss, recv_sem=rs, device_id=target, device_id_type=MESH
        )

    sent = []

    def put(src, dst, ss, rs, target, cond=None, own=None):
        def go():
            remote(src, dst, ss, rs, target).start()

        def fin():
            remote(src, dst, ss, rs, target).wait_send()

        conds = [] if cond is None else [cond]
        if own is not None:
            @pl.when(both(*conds, own))
            def _():
                pltpu.make_async_copy(src, dst, rs).start()

            conds.append(jnp.logical_not(own))
        if conds:
            pl.when(both(*conds))(go)
            sent.append((both(*conds), fin))
        else:
            go()
            sent.append((None, fin))

    def arrived(dst, rs, cond=None):
        def go():
            pltpu.make_async_copy(dst, dst, rs).wait()

        if cond is None:
            go()
        else:
            pl.when(cond)(go)

    def mslot(u, k):
        return mb.at[u, rows_of(k, 256)]

    def lslot(t, hf):
        return lb.at[rows_of(t * 2 + hf, 256)]

    def xslot(k):
        return xb.at[rows_of(k, 256)]

    barrier = pltpu.get_barrier_semaphore()
    for dv in range(8):
        for dq in range(4):
            if dv == 0 and dq == 0:
                continue
            tv = lax.rem(v + dv, 8)
            tq = lax.rem(q + dq, 4)
            to = (lax.div(tq, 2) * 4 + z) * 2 + lax.rem(tq, 2)
            pl.semaphore_signal(barrier, inc=1, device_id=(tv, to), device_id_type=MESH)
    for tz in zn:
        for tc in range(2):
            pl.semaphore_signal(barrier, inc=1, device_id=device(yh, x, yl, tz, tc), device_id_type=MESH)
    pl.semaphore_wait(barrier, 35)

    ls = lax.div(z, 2)
    lt = 2 * lax.rem(z, 2) + c
    for hf, d in ((0, 0), (1, 1), (1, 0), (0, 1)):
        put(lad.at[pl.ds(hf * 256, 256)], lslot(lt, hf), s_l.at[d, hf], r_l.at[lt, hf],
            device(yh, x, yl, zn[d], ls))
    ms = lax.div(x, 2)
    mu = lax.rem(x, 2)
    put(amp, mslot(mu, q), s_m.at[0], r_m.at[mu, q], device(yh, x, yh, z, ms),
        own=both(edge, c == ms))
    put(amp, tb, s_m.at[1], r_t, device(1 - yh, x, 1 - yl, z, c), cond=edge)
    put(amp, mslot(mu, q), s_m.at[1], r_m.at[mu, q], device(1 - yh, x, yh, z, ms),
        cond=jnp.logical_not(edge))
    for hf in range(2):
        put(lad.at[pl.ds(hf * 256, 256)], lslot(lt, hf), s_l.at[2, hf], r_l.at[lt, hf],
            device(yh, x, yl, z, ls), own=c == ls)
    put(xin.at[1 - yl], xslot(o), s_xa, r_x.at[o], device(yh, x, 1 - yl, z, c))
    pltpu.make_async_copy(xin.at[yl], xslot(o), r_x.at[o]).start()
    put(xin.at[yl], xslot(o), s_xd.at[0], r_x.at[o], device(yh, x, yl, z, 1 - c))

    origin = c == ms

    def spread_amplitudes(near):
        for e in range(2):
            k = near * 2 + e
            arrived(mslot(mu, k), r_m.at[mu, k], cond=origin)
            for d in range(2):
                put(mslot(mu, k), mslot(mu, k), s_mx.at[k, d], r_m.at[mu, k],
                    device(yh, xn[d], yl, z, c), cond=origin)

    spread_amplitudes(yh)

    arrived(tb, r_t, cond=edge)
    kt = (1 - yl) * 2 + c
    put(tb, mslot(mu, kt), s_mt, r_m.at[mu, kt], device(yh, x, 1 - yh, z, ms), cond=edge)

    spread_amplitudes(1 - yh)

    for u in range(2):
        dist = lax.rem(z - (2 * c + u) + 4, 4)
        for d in range(2):
            passing = dist == (1, 3)[d]
            for t in (2 * u, 2 * u + 1):
                arrived(lslot(t, d), r_l.at[t, d], cond=passing)
                put(lslot(t, d), lslot(t, d), s_lf.at[t, d], r_l.at[t, d],
                    device(yh, x, yl, zn[d], c), cond=passing)

    for d in range(2):
        put(xin.at[yl], xslot(o), s_xz.at[0, d], r_x.at[o], device(yh, x, yl, zn[d], c))
    op = ((1 - yl) * 4 + z) * 2 + c
    arrived(xslot(op), r_x.at[op])
    for d in range(2):
        put(xslot(op), xslot(op), s_xz.at[1, d], r_x.at[op], device(yh, x, yl, zn[d], c))
    put(xslot(op), xslot(op), s_xd.at[1], r_x.at[op], device(yh, x, yl, z, 1 - c))

    for near in (yh, 1 - yh):
        for u in range(2):
            dist = lax.rem(x - (2 * c + u) + 4, 4)
            for d in range(2):
                passing = dist == (1, 3)[d]
                k = near * 2 + d
                arrived(mslot(u, k), r_m.at[u, k], cond=passing)
                put(mslot(u, k), mslot(u, k), s_mf.at[u, k], r_m.at[u, k],
                    device(yh, xn[d], yl, z, c), cond=passing)

    lane = lax.broadcasted_iota(jnp.int32, (1, 1024), 1)
    slot_a = lax.div(lane, 64)
    slot_b = lax.rem(lane, 64)
    low = lax.broadcasted_iota(jnp.int32, (16, 128), 1) < 64
    low8 = lax.broadcasted_iota(jnp.int32, (8, 128), 1) < 64

    def rest_of_amplitudes(u):
        dist = lax.rem(x - (2 * c + u) + 4, 4)
        for k in range(4):
            done = jnp.logical_or(dist == 0, dist == (1, 3)[k % 2])
            arrived(mslot(u, k), r_m.at[u, k], cond=jnp.logical_not(done))

    def rest_of_ladder(u):
        dist = lax.rem(z - (2 * c + u) + 4, 4)
        for hf in range(2):
            for t in (2 * u, 2 * u + 1):
                arrived(lslot(t, hf), r_l.at[t, hf], cond=dist != (1, 3)[hf])

    def apply_mask(u):
        act = jnp.logical_and(slot_a + (32 * c + 16 * u) < cnt[2 * yl], slot_b < cnt[2 * yl + 1])
        mask = jnp.where(act, 1.0, 0.0).astype(BF16)

        @pl.loop(0, 32)
        def _(r):
            mm[u, rows_of(r, 32), :] = mb[u, rows_of(r, 32), :] * mask

    def reorder(u):
        @pl.loop(0, 8)
        def _(ap):
            @pl.loop(0, 16)
            def _(r):
                ff[rows_of(r, 64), :] = mm[u, rows_of(r, 64), rows_of(ap, 128)].astype(F32)

            for kp in range(32):
                v0 = ff[pl.ds(2 * kp, 16, stride=64), :]
                v1 = ff[pl.ds(2 * kp + 1, 16, stride=64), :]
                turned = pltpu.roll(jnp.where(low, v1, v0), 64, 1)
                pair = jnp.concatenate([jnp.where(low, v0, turned), jnp.where(low, turned, v1)], axis=0)
                rr[rows_of(u * 8 + ap, 32), kp * 128:(kp + 1) * 128] = pair.astype(BF16)

    def ladder_first(u):
        @pl.loop(0, 16)
        def _(t):
            rows, cols = rows_of(lax.div(t, 4), 256), rows_of(lax.rem(t, 4), 256)
            pp[rows, cols] = jnp.dot(mm[u, rows, :], lb[rows_of(u, 1024), cols], preferred_element_type=F32)

    def ladder_second(u, b, slot):
        @pl.loop(0, 4)
        def _(n):
            rows, cols = rows_of(b, 256), rows_of(n, 256)
            part = pp[rows, cols] + jnp.dot(
                mm[u, rows, :], lb[rows_of(u, 1024), cols], preferred_element_type=F32
            )
            if slot is None:
                pp[rows, cols] = part
            else:
                cs[slot, :, cols] = part.astype(BF16)

    def crossed(tz, first):
        @pl.loop(0, 2)
        def _(m):
            rows = rows_of(m, 256)
            for n in range(2):
                cols = slice(n * 256, (n + 1) * 256)
                part = jnp.dot(rr[rows, rows_of(tz, 512)], xb[rows_of(tz, 512), cols], preferred_element_type=F32)
                part += jnp.dot(
                    rr[rows, rows_of(4 + tz, 512)], xb[rows_of(4 + tz, 512), cols], preferred_element_type=F32
                )
                acc[rows, cols] = part if first else acc[rows, cols] + part

    def share_crossed(k, slot):
        put(xslot(k), xslot(k), s_xd.at[slot], r_x.at[k], device(yh, x, yl, z, 1 - c))

    def pass_crossed(b, slot):
        k = (b * 4 + lax.rem(z + 3 + 2 * b, 4)) * 2 + c
        arrived(xslot(k), r_x.at[k])
        put(xslot(k), xslot(k), s_xf.at[slot], r_x.at[k],
            device(yh, x, yl, lax.rem(z + 1 + 2 * b, 4), c))
        share_crossed(k, 2 + slot)

    u0 = jnp.where(origin, mu, 1 - mu)
    u1 = 1 - u0
    rest_of_amplitudes(u0)
    apply_mask(u0)
    reorder(u0)
    rest_of_ladder(u0)
    ladder_first(u0)
    pass_crossed(yl, 0)
    rest_of_amplitudes(u1)
    apply_mask(u1)
    rest_of_ladder(u1)

    ladder_second(u1, (1 - yl) * 2 + 1 - c, 0)
    put(cs.at[0], cr.at[0], s_c.at[0], r_c.at[0], device(yh, x, yl, z, 1 - c))
    ladder_second(u1, yl * 2 + 1 - c, 1)
    put(cs.at[1], cr.at[1], s_c.at[1], r_c.at[1], device(yh, x, yl, z, 1 - c))
    ladder_second(u1, (1 - yl) * 2 + c, None)
    arrived(cr.at[0], r_c.at[0])

    @pl.loop(0, 8)
    def _(r):
        part = pp[rows_of(((1 - yl) * 2 + c) * 8 + r, 32), :] + cr[0, rows_of(r, 32), :].astype(F32)
        cs[2, rows_of(r, 32), :] = part.astype(BF16)

    put(cs.at[2], cr.at[2], s_c.at[2], r_c.at[2], device(yh, x, 1 - yl, z, c))
    ladder_second(u1, q, None)
    pass_crossed(1 - yl, 1)
    reorder(u1)

    for d in range(2):
        k = ((1 - d) * 4 + zn[1 - d]) * 2 + c
        arrived(xslot(k), r_x.at[k])
        share_crossed(k, 4 + d)
    arrived(xslot(o), r_x.at[o])

    def other_core(tz):
        for b in range(2):
            k = (b * 4 + tz) * 2 + 1 - c
            arrived(xslot(k), r_x.at[k])

    other_core(z)
    crossed(z, True)
    for b in range(2):
        k = (b * 4 + zo) * 2 + c
        arrived(xslot(k), r_x.at[k])
        share_crossed(k, 6 + b)
    for tz in (zn[0], zn[1], zo):
        other_core(tz)
        crossed(tz, False)

    def back():
        @pl.loop(0, 16)
        def _(ap):
            for jp in range(4):
                cols = slice(jp * 128, (jp + 1) * 128)
                for ih in range(2):
                    v0 = acc[rows_of(ap * 4 + ih, 8), cols]
                    v1 = acc[rows_of(ap * 4 + 2 + ih, 8), cols]
                    turned = pltpu.roll(jnp.where(low8, v1, v0), 64, 1)
                    dd[ap, pl.ds(ih * 64 + 2 * jp, 8, stride=8), :] = jnp.where(low8, v0, turned)
                    dd[ap, pl.ds(ih * 64 + 2 * jp + 1, 8, stride=8), :] = jnp.where(low8, turned, v1)

    back()
    for u in range(2):
        for k in range(4):
            for ap in range(8):
                xs[u * 4 + k, :, ap * 128:(ap + 1) * 128] = dd[u * 8 + ap, k * 32:(k + 1) * 32, :].astype(BF16)
            put(xs.at[u * 4 + k], xr.at[v], s_o.at[u * 4 + k], r_o.at[v],
                device(yl, 2 * c + u, k // 2, z, k % 2),
                own=both(yh == yl, x == 2 * c + u, yl == k // 2, c == k % 2))

    arrived(cr.at[1], r_c.at[1])
    arrived(cr.at[2], r_c.at[2])

    @pl.loop(0, 8)
    def _(r):
        rows = rows_of(q * 8 + r, 32)
        pp[rows, :] = pp[rows, :] + (cr[1, rows_of(r, 32), :].astype(F32) + cr[2, rows_of(r, 32), :].astype(F32))

    act_out = jnp.logical_and(slot_a + 16 * x < cnt[2 * yh], slot_b < cnt[2 * yh + 1])
    mask_out = jnp.where(act_out, 1.0, 0.0).astype(F32)
    for k in range(8):
        arrived(xr.at[k], r_o.at[k])
        got = xr[k].astype(F32)
        for i in range(4):
            rows = rows_of(q * 32 + i * 8 + k, 8)
            pp[rows, :] = (pp[rows, :] + got[i * 8:(i + 1) * 8]) * mask_out

    @pl.loop(0, 8)
    def _(r):
        out[rows_of(r, 32), :] = pp[rows_of(q * 8 + r, 32), :].astype(BF16)

    for cond, fin in sent:
        if cond is None:
            fin()
        else:
            pl.when(cond)(fin)


def per_device(amplitudes, ladder_integrals, crossed_integrals, vir_counts):
    dma = pltpu.SemaphoreType.DMA
    hbm = pl.BlockSpec(memory_space=pl.ANY)
    return pl.pallas_call(
        kernel,
        out_shape=jax.ShapeDtypeStruct((256, 1024), BF16),
        in_specs=[pl.BlockSpec(memory_space=pltpu.SMEM), hbm, hbm, hbm],
        out_specs=pl.BlockSpec(memory_space=pltpu.VMEM),
        scratch_shapes=[
            pltpu.VMEM((2, 1024, 1024), BF16),
            pltpu.VMEM((2048, 1024), BF16),
            pltpu.VMEM((4096, 512), BF16),
            pltpu.VMEM((256, 1024), BF16),
            pltpu.VMEM((2, 1024, 1024), BF16),
            pltpu.VMEM((1024, 1024), F32),
            pltpu.VMEM((512, 4096), BF16),
            pltpu.VMEM((1024, 128), F32),
            pltpu.VMEM((512, 512), F32),
            pltpu.VMEM((16, 128, 128), F32),
            pltpu.VMEM((3, 256, 1024), BF16),
            pltpu.VMEM((3, 256, 1024), BF16),
            pltpu.VMEM((8, 32, 1024), BF16),
            pltpu.VMEM((8, 32, 1024), BF16),
            dma((3, 2)), dma((4, 2)), dma((2,)), dma, dma((4, 2)), dma((2, 4)),
            dma, dma((8,)), dma((2, 2)), dma((2,)), dma((3,)), dma((8,)),
            dma((2, 4)), dma, dma((4, 2)), dma((16,)), dma((3,)), dma((8,)),
        ],
        compiler_params=pltpu.CompilerParams(
            collective_id=0, has_side_effects=True, vmem_limit_bytes=56 * 1024 * 1024
        ),
        name="residual",
    )(vir_counts, amplitudes, ladder_integrals, crossed_integrals)


def solution(mesh):
    in_specs = (P("occ", "vir"), P("occ", "vir"), P(None, "occ", "vir"), P())
    return jax.shard_map(
        per_device, mesh=mesh, in_specs=in_specs, out_specs=P("occ", "vir"), check_vma=False
    )
```

```python
import jax
import jax.numpy as jnp
from jax import lax
from jax.experimental import pallas as pl
from jax.experimental.pallas import tpu as pltpu
from jax.sharding import PartitionSpec as P

MESH = pl.DeviceIdType.MESH
F32 = jnp.float32
BF16 = jnp.bfloat16
NP = 4


def both(*conds):
    out = conds[0]
    for other in conds[1:]:
        out = jnp.logical_and(out, other)
    return out


def device(yh, x, yl, z, c):
    return (yh * 4 + x, (yl * 4 + z) * 2 + c)


def rows_of(k, size):
    return pl.ds(pl.multiple_of(k * size, size), size)


def kernel(
    cnt, amp, lad, xin, out,
    mb, lb, xb, tb, mm, pp, rr, ff, acc, dd, cs, cr, xs, xr,
    s_l, s_lf, s_m, s_mt, s_mx, s_mf, s_xa, s_xd, s_xz, s_xf, s_c, s_o,
    r_m, r_t, r_l, r_x, r_c, r_o,
):
    v = lax.axis_index("vir")
    o = lax.axis_index("occ")
    yh = lax.div(v, 4)
    x = lax.rem(v, 4)
    yl = lax.div(o, 8)
    z = lax.rem(lax.div(o, 2), 4)
    c = lax.rem(o, 2)
    xn = (lax.rem(x + 1, 4), lax.rem(x + 3, 4))
    zn = (lax.rem(z + 1, 4), lax.rem(z + 3, 4))
    zo = lax.rem(z + 2, 4)
    q = yl * 2 + c
    edge = yh == yl
    inner = jnp.logical_not(edge)

    def put(src, dst, ss, rs, target, cond=None, own=None):
        def go():
            pltpu.make_async_remote_copy(
                src_ref=src, dst_ref=dst, send_sem=ss, recv_sem=rs, device_id=target, device_id_type=MESH
            ).start()

        if own is not None:
            @pl.when(own)
            def _():
                pltpu.make_async_copy(src, dst, rs).start()

            cond = jnp.logical_not(own)
        if cond is None:
            go()
        else:
            pl.when(cond)(go)

    def arrived(ref, sem, cond=None):
        def go():
            pltpu.make_async_copy(ref, ref, sem).wait()

        if cond is None:
            go()
        else:
            pl.when(cond)(go)

    PR = 256 // NP

    def mslot(u, k, p):
        return mb.at[u, rows_of(k * NP + p, PR)]

    def lslot(t, hf):
        return lb.at[rows_of(t * 2 + hf, 256)]

    def xslot(h, k):
        return xb.at[h, rows_of(k, 256)]

    def xpart(g, h):
        return xin.at[g, :, pl.ds(h * 256, 256)]

    barrier = pltpu.get_barrier_semaphore()
    for dv in range(8):
        for dq in range(4):
            if dv == 0 and dq == 0:
                continue
            tv = lax.rem(v + dv, 8)
            tq = lax.rem(q + dq, 4)
            to = (lax.div(tq, 2) * 4 + z) * 2 + lax.rem(tq, 2)
            pl.semaphore_signal(barrier, inc=1, device_id=(tv, to), device_id_type=MESH)
    for tz in zn:
        for tc in range(2):
            pl.semaphore_signal(barrier, inc=1, device_id=device(yh, x, yl, tz, tc), device_id_type=MESH)
    pl.semaphore_wait(barrier, 35)

    ls = lax.div(z, 2)
    lt = 2 * lax.rem(z, 2) + c
    for hf, d in ((0, 0), (1, 1), (1, 0), (0, 1)):
        put(lad.at[pl.ds(hf * 256, 256)], lslot(lt, hf), s_l.at[d], r_l.at[lt, hf],
            device(yh, x, yl, zn[d], ls))
    ms = lax.div(x, 2)
    mu = lax.rem(x, 2)
    for p in range(NP):
        part = amp.at[pl.ds(p * PR, PR)]
        put(part, mslot(mu, q, p), s_m.at[0], r_m.at[mu, q, p], device(yh, x, yh, z, ms),
            own=both(edge, c == ms))
        put(part, tb.at[pl.ds(p * PR, PR)], s_m.at[1], r_t.at[p], device(1 - yh, x, 1 - yl, z, c),
            cond=edge)
        put(part, mslot(mu, q, p), s_m.at[1], r_m.at[mu, q, p], device(1 - yh, x, yh, z, ms),
            cond=inner)
    for h in range(2):
        put(xpart(1 - yl, h), xslot(h, o), s_xa, r_x.at[h, o], device(yh, x, 1 - yl, z, c))
    for hf in range(2):
        put(lad.at[pl.ds(hf * 256, 256)], lslot(lt, hf), s_l.at[2], r_l.at[lt, hf],
            device(yh, x, yl, z, ls), own=c == ls)
    for h in range(2):
        pltpu.make_async_copy(xpart(yl, h), xslot(h, o), r_x.at[h, o]).start()
        put(xpart(yl, h), xslot(h, o), s_xd.at[h], r_x.at[h, o], device(yh, x, yl, z, 1 - c))

    origin = c == ms

    def spread_amplitudes(k, p):
        arrived(mslot(mu, k, p), r_m.at[mu, k, p], cond=origin)
        for d in range(2):
            put(mslot(mu, k, p), mslot(mu, k, p), s_mx.at[d], r_m.at[mu, k, p],
                device(yh, xn[d], yl, z, c), cond=origin)

    for p in range(NP):
        for e in range(2):
            spread_amplitudes(yh * 2 + e, p)
    kt = (1 - yl) * 2 + c
    for p in range(NP):
        part = tb.at[pl.ds(p * PR, PR)]
        arrived(part, r_t.at[p], cond=edge)
        put(part, mslot(mu, kt, p), s_mt, r_m.at[mu, kt, p], device(yh, x, 1 - yh, z, ms), cond=edge)
        for e in range(2):
            spread_amplitudes((1 - yh) * 2 + e, p)

    ldist = [lax.rem(z - (2 * c + u) + 4, 4) for u in range(2)]
    for u in range(2):
        for d in range(2):
            passing = ldist[u] == (1, 3)[d]
            for t in (2 * u, 2 * u + 1):
                arrived(lslot(t, d), r_l.at[t, d], cond=passing)
                put(lslot(t, d), lslot(t, d), s_lf, r_l.at[t, d],
                    device(yh, x, yl, zn[d], c), cond=passing)

    op = ((1 - yl) * 4 + z) * 2 + c

    def send_own(h):
        for d in range(2):
            put(xpart(yl, h), xslot(h, o), s_xz.at[h, d], r_x.at[h, o], device(yh, x, yl, zn[d], c))

    def share_crossed(h, k):
        put(xslot(h, k), xslot(h, k), s_xd.at[h], r_x.at[h, k], device(yh, x, yl, z, 1 - c))

    def send_other(h):
        arrived(xslot(h, op), r_x.at[h, op])
        for d in range(2):
            put(xslot(h, op), xslot(h, op), s_xz.at[h, d], r_x.at[h, op], device(yh, x, yl, zn[d], c))
        share_crossed(h, op)

    def pass_crossed(h, b):
        k = (b * 4 + lax.rem(z + 3 + 2 * b, 4)) * 2 + c
        arrived(xslot(h, k), r_x.at[h, k])
        put(xslot(h, k), xslot(h, k), s_xf.at[h], r_x.at[h, k],
            device(yh, x, yl, lax.rem(z + 1 + 2 * b, 4), c))
        share_crossed(h, k)

    def take_near(h):
        for d in range(2):
            k = ((1 - d) * 4 + zn[1 - d]) * 2 + c
            arrived(xslot(h, k), r_x.at[h, k])
            share_crossed(h, k)

    def take_far(h):
        for b in range(2):
            k = (b * 4 + zo) * 2 + c
            arrived(xslot(h, k), r_x.at[h, k])
            share_crossed(h, k)

    def other_core(h, tz):
        for b in range(2):
            k = (b * 4 + tz) * 2 + 1 - c
            arrived(xslot(h, k), r_x.at[h, k])

    send_own(0)
    send_other(0)
    send_own(1)

    lane = lax.broadcasted_iota(jnp.int32, (1, 1024), 1)
    slot_a = lax.div(lane, 64)
    slot_b = lax.rem(lane, 64)
    low = lax.broadcasted_iota(jnp.int32, (16, 128), 1) < 64
    low8 = lax.broadcasted_iota(jnp.int32, (8, 128), 1) < 64

    def rest_of_amplitudes(u):
        dist = lax.rem(x - (2 * c + u) + 4, 4)
        for k in range(4):
            done = jnp.logical_or(dist == 0, dist == (1, 3)[k % 2])
            for p in range(NP):
                arrived(mslot(u, k, p), r_m.at[u, k, p], cond=jnp.logical_not(done))

    def rest_of_ladder(u):
        dist = lax.rem(z - (2 * c + u) + 4, 4)
        for hf in range(2):
            for t in (2 * u, 2 * u + 1):
                arrived(lslot(t, hf), r_l.at[t, hf], cond=dist != (1, 3)[hf])

    def apply_mask(u):
        act = jnp.logical_and(slot_a + (32 * c + 16 * u) < cnt[2 * yl], slot_b < cnt[2 * yl + 1])
        mask = jnp.where(act, 1.0, 0.0).astype(BF16)

        @pl.loop(0, 32)
        def _(r):
            mm[u, rows_of(r, 32), :] = mb[u, rows_of(r, 32), :] * mask

    def reorder(u):
        @pl.loop(0, 8)
        def _(ap):
            @pl.loop(0, 16)
            def _(r):
                ff[pl.ds(pl.multiple_of(r * 72, 8), 64), :] = mm[u, rows_of(r, 64), rows_of(ap, 128)].astype(F32)

            for kp in range(32):
                v0 = ff[pl.ds(2 * kp, 16, stride=72), :]
                v1 = ff[pl.ds(2 * kp + 1, 16, stride=72), :]
                turned = pltpu.roll(jnp.where(low, v1, v0), 64, 1)
                pair = jnp.concatenate([jnp.where(low, v0, turned), jnp.where(low, turned, v1)], axis=0)
                rr[rows_of(u * 8 + ap, 32), kp * 128:(kp + 1) * 128] = pair.astype(BF16)

    def ladder_first(u):
        @pl.loop(0, 16)
        def _(t):
            rows, cols = rows_of(lax.div(t, 4), 256), rows_of(lax.rem(t, 4), 256)
            pp[rows, cols] = jnp.dot(mm[u, rows, :], lb[rows_of(u, 1024), cols], preferred_element_type=F32)

    def ladder_second(u, b, slot):
        @pl.loop(0, 4)
        def _(n):
            rows, cols = rows_of(b, 256), rows_of(n, 256)
            part = pp[rows, cols] + jnp.dot(
                mm[u, rows, :], lb[rows_of(u, 1024), cols], preferred_element_type=F32
            )
            if slot is None:
                pp[rows, cols] = part
            else:
                cs[slot, :, cols] = part.astype(BF16)

    def crossed(h, tz, first):
        @pl.loop(0, 2)
        def _(m):
            rows = rows_of(m, 256)
            part = jnp.dot(rr[rows, rows_of(tz, 512)], xb[h, rows_of(tz, 512), :], preferred_element_type=F32)
            part += jnp.dot(
                rr[rows, rows_of(4 + tz, 512)], xb[h, rows_of(4 + tz, 512), :], preferred_element_type=F32
            )
            acc[rows, :] = part if first else acc[rows, :] + part

    def back(u):
        @pl.loop(0, 8)
        def _(ap):
            for jp in range(2):
                cols = slice(jp * 128, (jp + 1) * 128)
                for ih in range(2):
                    v0 = acc[rows_of((u * 8 + ap) * 4 + ih, 8), cols]
                    v1 = acc[rows_of((u * 8 + ap) * 4 + 2 + ih, 8), cols]
                    turned = pltpu.roll(jnp.where(low8, v1, v0), 64, 1)
                    dd[ap, pl.ds(ih * 32 + 2 * jp, 8, stride=4), :] = jnp.where(low8, v0, turned)
                    dd[ap, pl.ds(ih * 32 + 2 * jp + 1, 8, stride=4), :] = jnp.where(low8, turned, v1)

    own_out = both(edge, origin)

    def give_back(h):
        for u in range(2):
            back(u)
            for k in range(4):
                for ap in range(8):
                    xs[h, u * 4 + k, :, ap * 128:(ap + 1) * 128] = dd[ap, k * 16:(k + 1) * 16, :].astype(BF16)
                put(xs.at[h, u * 4 + k], xr.at[h, v], s_o.at[h], r_o.at[h, v],
                    device(yl, 2 * c + u, k // 2, z, k % 2),
                    own=both(own_out, mu == u, q == k))

    u0 = jnp.where(origin, mu, 1 - mu)
    u1 = 1 - u0

    def prepare(u):
        apply_mask(u)
        reorder(u)

    @pl.when(origin)
    def _():
        prepare(u0)

    for near in (yh, 1 - yh):
        for p in range(NP):
            for u in range(2):
                dist = lax.rem(x - (2 * c + u) + 4, 4)
                for d in range(2):
                    passing = dist == (1, 3)[d]
                    k = near * 2 + d
                    arrived(mslot(u, k, p), r_m.at[u, k, p], cond=passing)
                    put(mslot(u, k, p), mslot(u, k, p), s_mf, r_m.at[u, k, p],
                        device(yh, xn[d], yl, z, c), cond=passing)

    @pl.when(jnp.logical_not(origin))
    def _():
        rest_of_amplitudes(u0)
        prepare(u0)

    rest_of_ladder(u0)
    ladder_first(u0)
    pass_crossed(0, yl)
    rest_of_amplitudes(u1)
    apply_mask(u1)
    rest_of_ladder(u1)

    ladder_second(u1, (1 - yl) * 2 + 1 - c, 0)
    put(cs.at[0], cr.at[0], s_c.at[0], r_c.at[0], device(yh, x, yl, z, 1 - c))
    ladder_second(u1, yl * 2 + 1 - c, 1)
    put(cs.at[1], cr.at[1], s_c.at[1], r_c.at[1], device(yh, x, yl, z, 1 - c))
    pass_crossed(0, 1 - yl)
    send_other(1)
    ladder_second(u1, (1 - yl) * 2 + c, None)
    arrived(cr.at[0], r_c.at[0])

    @pl.loop(0, 8)
    def _(r):
        part = pp[rows_of(((1 - yl) * 2 + c) * 8 + r, 32), :] + cr[0, rows_of(r, 32), :].astype(F32)
        cs[2, rows_of(r, 32), :] = part.astype(BF16)

    put(cs.at[2], cr.at[2], s_c.at[2], r_c.at[2], device(yh, x, 1 - yl, z, c))
    ladder_second(u1, q, None)
    pass_crossed(1, yl)
    take_near(0)
    reorder(u1)
    pass_crossed(1, 1 - yl)
    take_far(0)

    for h in range(2):
        arrived(xslot(h, o), r_x.at[h, o])
        for tz in (z, zn[0], zn[1], zo):
            if h == 1 and tz is zn[0]:
                take_near(1)
            if h == 1 and tz is zo:
                take_far(1)
            other_core(h, tz)
            crossed(h, tz, tz is z)
        give_back(h)

    arrived(cr.at[1], r_c.at[1])
    arrived(cr.at[2], r_c.at[2])
    act_out = jnp.logical_and(slot_a + 16 * x < cnt[2 * yh], slot_b < cnt[2 * yh + 1])
    mask_out = jnp.where(act_out, 1.0, 0.0).astype(F32)

    @pl.loop(0, 8)
    def _(r):
        rows = rows_of(q * 8 + r, 32)
        pp[rows, :] = pp[rows, :] + (cr[1, rows_of(r, 32), :].astype(F32) + cr[2, rows_of(r, 32), :].astype(F32))

    for d in range(3):
        arrived(lad, s_l.at[d], cond=None if d < 2 else c != ls)
    lpass = [jnp.logical_or(ldist[u] == 1, ldist[u] == 3) for u in range(2)]
    for u in range(2):
        arrived(lb.at[pl.ds(0, 512)], s_lf, cond=lpass[u])
    arrived(amp, s_m.at[0], cond=jnp.logical_not(own_out))
    arrived(amp, s_m.at[1])
    arrived(tb, s_mt, cond=edge)
    for d in range(2):
        arrived(mb.at[0], s_mx.at[d], cond=origin)
    arrived(mb.at[0, pl.ds(0, 512)], s_mf)
    arrived(xb.at[pl.ds(0, 2), pl.ds(0, 256)], s_xa)
    for h in range(2):
        arrived(xb.at[h, pl.ds(0, 2048)], s_xd.at[h])
        arrived(xb.at[h, pl.ds(0, 512)], s_xf.at[h])
        for d in range(2):
            arrived(xb.at[h, pl.ds(0, 512)], s_xz.at[h, d])
    for k in range(3):
        arrived(cs.at[k], s_c.at[k])

    for kk in range(4):
        got = []
        for k in (2 * kk, 2 * kk + 1):
            for h in range(2):
                arrived(xr.at[h, k], r_o.at[h, k])
            got.append([xr[h, k].astype(F32) for h in range(2)])
        for i in range(4):
            part = jnp.concatenate([g[h][i * 4:i * 4 + 4] for g in got for h in range(2)], axis=0)
            rows = rows_of(q * 16 + i * 4 + kk, 16)
            out[i * 64 + kk * 16:i * 64 + kk * 16 + 16, :] = ((pp[rows, :] + part) * mask_out).astype(BF16)

    for h in range(2):
        arrived(xs.at[h], s_o.at[h], cond=jnp.logical_not(own_out))
        arrived(xs.at[h, pl.ds(0, 7)], s_o.at[h], cond=own_out)


def per_device(amplitudes, ladder_integrals, crossed_integrals, vir_counts):
    dma = pltpu.SemaphoreType.DMA
    hbm = pl.BlockSpec(memory_space=pl.ANY)
    return pl.pallas_call(
        kernel,
        out_shape=pltpu.VMEM((256, 1024), BF16),
        in_specs=[pl.BlockSpec(memory_space=pltpu.SMEM), hbm, hbm, hbm],
        out_specs=pl.BlockSpec(memory_space=pltpu.VMEM),
        scratch_shapes=[
            pltpu.VMEM((2, 1024, 1024), BF16),
            pltpu.VMEM((2048, 1024), BF16),
            pltpu.VMEM((2, 4096, 256), BF16),
            pltpu.VMEM((256, 1024), BF16),
            pltpu.VMEM((2, 1024, 1024), BF16),
            pltpu.VMEM((1024, 1024), F32),
            pltpu.VMEM((512, 4096), BF16),
            pltpu.VMEM((1152, 128), F32),
            pltpu.VMEM((512, 256), F32),
            pltpu.VMEM((8, 64, 128), F32),
            pltpu.VMEM((3, 256, 1024), BF16),
            pltpu.VMEM((3, 256, 1024), BF16),
            pltpu.VMEM((2, 8, 16, 1024), BF16),
            pltpu.VMEM((2, 8, 16, 1024), BF16),
            dma((3,)), dma, dma((2,)), dma, dma((2,)), dma,
            dma, dma((2,)), dma((2, 2)), dma((2,)), dma((3,)), dma((2,)),
            dma((2, 4, NP)), dma((NP,)), dma((4, 2)), dma((2, 16)), dma((3,)), dma((2, 8)),
        ],
        compiler_params=pltpu.CompilerParams(
            collective_id=0, has_side_effects=True, vmem_limit_bytes=56 * 1024 * 1024
        ),
        name="residual",
    )(vir_counts, amplitudes, ladder_integrals, crossed_integrals)


def solution(mesh):
    in_specs = (P("occ", "vir"), P("occ", "vir"), P(None, "occ", "vir"), P())
    return jax.shard_map(
        per_device, mesh=mesh, in_specs=in_specs, out_specs=P("occ", "vir"), check_vma=False
    )
```

```python
import jax
import jax.numpy as jnp
from jax import lax
from jax.experimental import pallas as pl
from jax.experimental.pallas import tpu as pltpu
from jax.sharding import PartitionSpec as P

MESH = pl.DeviceIdType.MESH
F32 = jnp.float32
BF16 = jnp.bfloat16
NP = 4


def both(*conds):
    out = conds[0]
    for other in conds[1:]:
        out = jnp.logical_and(out, other)
    return out


def device(yh, x, yl, z, c):
    return (yh * 4 + x, (yl * 4 + z) * 2 + c)


def rows_of(k, size):
    return pl.ds(pl.multiple_of(k * size, size), size)


def kernel(
    cnt, amp, lad, xin, out,
    mb, lb, xb, tb, xt, tt, mm, pp, rr, ff, acc, dd, cs, cr, xs, xr,
    s_l, s_lf, s_m, s_mt, s_mx, s_mf, s_t, s_tf, s_y, s_xa, s_xd, s_xz, s_xf, s_c, s_o,
    r_m, r_t, r_xt, r_tt, r_l, r_lf, r_x, r_c, r_o,
):
    v = lax.axis_index("vir")
    o = lax.axis_index("occ")
    yh = lax.div(v, 4)
    x = lax.rem(v, 4)
    yl = lax.div(o, 8)
    z = lax.rem(lax.div(o, 2), 4)
    c = lax.rem(o, 2)
    xn = (lax.rem(x + 1, 4), lax.rem(x + 3, 4))
    zn = (lax.rem(z + 1, 4), lax.rem(z + 3, 4))
    zo = lax.rem(z + 2, 4)
    q = yl * 2 + c
    edge = yh == yl
    inner = jnp.logical_not(edge)

    def put(src, dst, ss, rs, target, cond=None, own=None):
        def go():
            pltpu.make_async_remote_copy(
                src_ref=src, dst_ref=dst, send_sem=ss, recv_sem=rs, device_id=target, device_id_type=MESH
            ).start()

        if own is not None:
            @pl.when(own)
            def _():
                pltpu.make_async_copy(src, dst, rs).start()

            cond = jnp.logical_not(own)
        if cond is None:
            go()
        else:
            pl.when(cond)(go)

    def arrived(ref, sem, cond=None):
        def go():
            pltpu.make_async_copy(ref, ref, sem).wait()

        if cond is None:
            go()
        else:
            pl.when(cond)(go)

    PR = 256 // NP

    def mslot(u, k, p):
        return mb.at[u, rows_of(k * NP + p, PR)]

    def lslot(t, hf):
        return lb.at[rows_of(t * 2 + hf, 256)]

    def xslot(k):
        return xb.at[rows_of(k, 256)]

    barrier = pltpu.get_barrier_semaphore()
    for dv in range(8):
        for dq in range(4):
            if dv == 0 and dq == 0:
                continue
            tv = lax.rem(v + dv, 8)
            tq = lax.rem(q + dq, 4)
            to = (lax.div(tq, 2) * 4 + z) * 2 + lax.rem(tq, 2)
            pl.semaphore_signal(barrier, inc=1, device_id=(tv, to), device_id_type=MESH)
    for tz in zn:
        for tc in range(2):
            pl.semaphore_signal(barrier, inc=1, device_id=device(yh, x, yl, tz, tc), device_id_type=MESH)
    pl.semaphore_wait(barrier, 35)

    put(xin.at[1 - yl], xslot(o), s_xa, r_x.at[o], device(yh, x, 1 - yl, z, c))
    for d in range(2):
        put(xin.at[yl], xslot(o), s_xz.at[d], r_x.at[o], device(yh, x, yl, zn[d], c))
    ms = lax.div(x, 2)
    mu = lax.rem(x, 2)
    LP = NP - 1
    for d in range(2):
        put(amp.at[pl.ds(LP * PR, PR)], xt.at[d], s_t.at[d], r_xt.at[d], device(yh, xn[d], yl, z, c))
    for p in range(NP):
        part = amp.at[pl.ds(p * PR, PR)]
        put(part, mslot(mu, q, p), s_m.at[0], r_m.at[mu, q, p], device(yh, x, yh, z, ms),
            own=both(edge, c == ms))
        put(part, tb.at[pl.ds(p * PR, PR)], s_m.at[1], r_t.at[p], device(1 - yh, x, 1 - yl, z, c),
            cond=edge)
        put(part, mslot(mu, q, p), s_m.at[1], r_m.at[mu, q, p], device(1 - yh, x, yh, z, ms),
            cond=inner)
    pltpu.make_async_copy(xin.at[yl], xslot(o), r_x.at[o]).start()

    def share_crossed(k, src=None):
        put(xslot(k) if src is None else src, xslot(k), s_xd, r_x.at[k], device(yh, x, yl, z, 1 - c))

    share_crossed(o, xin.at[yl])
    ls = lax.div(z, 2)
    lt = 2 * lax.rem(z, 2) + c
    for hf in range(2):
        put(lad.at[pl.ds(hf * 256, 256)], lslot(lt, hf), s_l.at[2], r_l.at[lt, hf],
            device(yh, x, yl, z, ls), own=c == ls)

    op = ((1 - yl) * 4 + z) * 2 + c
    arrived(xslot(op), r_x.at[op])
    for d in range(2):
        put(xslot(op), xslot(op), s_xz.at[d], r_x.at[op], device(yh, x, yl, zn[d], c))

    def send_ladder(part):
        for d in range(2):
            hf = d if part == 0 else 1 - d
            put(lad.at[pl.ds(hf * 256, 256)], lslot(lt, hf), s_l.at[d], r_l.at[lt, hf],
                device(yh, x, yl, zn[d], ls))

    send_ladder(0)
    share_crossed(op)

    xsrc = (xn[1], xn[0], lax.rem(x + 2, 4))

    def along_y(i):
        xs_, part = xsrc[i], xt.at[i]
        arrived(part, r_xt.at[i])
        u, core = lax.rem(xs_, 2), lax.div(xs_, 2)
        put(part, mslot(u, q, LP), s_y.at[0, i], r_m.at[u, q, LP], device(yh, x, yh, z, core),
            own=both(edge, c == core))
        put(part, tt.at[i], s_y.at[1, i], r_tt.at[i], device(1 - yh, x, 1 - yl, z, c), cond=edge)
        put(part, mslot(u, q, LP), s_y.at[1, i], r_m.at[u, q, LP], device(1 - yh, x, yh, z, core),
            cond=inner)

    for i in range(2):
        along_y(i)
        put(xt.at[i], xt.at[2], s_tf, r_xt.at[2], device(yh, xn[i], yl, z, c), cond=c == i)

    origin = c == ms

    def spread_amplitudes(k, p):
        arrived(mslot(mu, k, p), r_m.at[mu, k, p], cond=origin)
        for d in range(2):
            put(mslot(mu, k, p), mslot(mu, k, p), s_mx.at[d], r_m.at[mu, k, p],
                device(yh, xn[d], yl, z, c), cond=origin)

    for p in range(LP):
        for e in range(2):
            spread_amplitudes(yh * 2 + e, p)

    def pass_crossed(b):
        k = (b * 4 + lax.rem(z + 3 + 2 * b, 4)) * 2 + c
        arrived(xslot(k), r_x.at[k])
        put(xslot(k), xslot(k), s_xf, r_x.at[k], device(yh, x, yl, lax.rem(z + 1 + 2 * b, 4), c))
        share_crossed(k)

    pass_crossed(yl)
    pass_crossed(1 - yl)
    send_ladder(1)
    for d in range(2):
        k = ((1 - d) * 4 + zn[1 - d]) * 2 + c
        arrived(xslot(k), r_x.at[k])
        share_crossed(k)

    along_y(2)

    kt = (1 - yl) * 2 + c
    for p in range(NP):
        part = tb.at[pl.ds(p * PR, PR)]
        arrived(part, r_t.at[p], cond=edge)
        put(part, mslot(mu, kt, p), s_mt, r_m.at[mu, kt, p], device(yh, x, 1 - yh, z, ms), cond=edge)
        if p < LP:
            for e in range(2):
                spread_amplitudes((1 - yh) * 2 + e, p)

    lane = lax.broadcasted_iota(jnp.int32, (1, 1024), 1)
    slot_a = lax.div(lane, 64)
    slot_b = lax.rem(lane, 64)
    low = lax.broadcasted_iota(jnp.int32, (16, 128), 1) < 64
    low8 = lax.broadcasted_iota(jnp.int32, (8, 128), 1) < 64

    def rest_of_amplitudes(u):
        dist = lax.rem(x - (2 * c + u) + 4, 4)
        for k in range(4):
            done = jnp.logical_or(dist == 0, dist == (1, 3)[k % 2])
            for p in range(LP):
                arrived(mslot(u, k, p), r_m.at[u, k, p], cond=jnp.logical_not(done))
            arrived(mslot(u, k, LP), r_m.at[u, k, LP])

    ldist = [lax.rem(z - (2 * c + u) + 4, 4) for u in range(2)]
    e1 = jnp.where(ldist[0] == 2, 0, 1)
    e0 = 1 - e1

    def rest_of_ladder(e):
        dist = lax.rem(z - (2 * c + e) + 4, 4)
        for hf in range(2):
            for t in range(2):
                arrived(lslot(2 * e + t, hf), r_l.at[2 * e + t, hf],
                        cond=both(dist != (1, 3)[hf], dist != 2))

    def lchunk(t, hf, j):
        return lb.at[rows_of(t * 2 + hf, 256), pl.ds(j * 256, 256)]

    def far_ladder(j):
        for hf in range(2):
            for t in range(2):
                arrived(lchunk(2 * e1 + t, hf, j), r_lf.at[2 * e1 + t, hf, j],
                        cond=lax.rem(z - (2 * c + e1) + 4, 4) == 2)

    def pass_ladder():
        for u in range(2):
            for d in range(2):
                for t in (2 * u, 2 * u + 1):
                    arrived(lslot(t, d), r_l.at[t, d], cond=ldist[u] == (1, 3)[d])
        for j in range(4):
            for u in range(2):
                for d in range(2):
                    for t in (2 * u, 2 * u + 1):
                        put(lchunk(t, d, j), lchunk(t, d, j), s_lf, r_lf.at[t, d, j],
                            device(yh, x, yl, zn[d], c), cond=ldist[u] == (1, 3)[d])

    def apply_mask(u):
        act = jnp.logical_and(slot_a + (32 * c + 16 * u) < cnt[2 * yl], slot_b < cnt[2 * yl + 1])
        mask = jnp.where(act, 1.0, 0.0).astype(BF16)

        @pl.loop(0, 32)
        def _(r):
            mm[u, rows_of(r, 32), :] = mb[u, rows_of(r, 32), :] * mask

    def reorder(u):
        @pl.loop(0, 8)
        def _(ap):
            @pl.loop(0, 16)
            def _(r):
                ff[pl.ds(pl.multiple_of(r * 72, 8), 64), :] = mm[u, rows_of(r, 64), rows_of(ap, 128)].astype(F32)

            for kp in range(32):
                v0 = ff[pl.ds(2 * kp, 16, stride=72), :]
                v1 = ff[pl.ds(2 * kp + 1, 16, stride=72), :]
                turned = pltpu.roll(jnp.where(low, v1, v0), 64, 1)
                pair = jnp.concatenate([jnp.where(low, v0, turned), jnp.where(low, turned, v1)], axis=0)
                rr[rows_of(u * 8 + ap, 32), kp * 128:(kp + 1) * 128] = pair.astype(BF16)

    def ladder_first(u, j):
        @pl.loop(0, 4)
        def _(t):
            rows, cols = rows_of(t, 256), slice(j * 256, (j + 1) * 256)
            pp[rows, cols] = jnp.dot(mm[u, rows, :], lb[rows_of(u, 1024), cols], preferred_element_type=F32)

    def ladder_second(u, j, b, slot):
        rows, cols = rows_of(b, 256), slice(j * 256, (j + 1) * 256)
        part = pp[rows, cols] + jnp.dot(mm[u, rows, :], lb[rows_of(u, 1024), cols], preferred_element_type=F32)
        if slot is None:
            pp[rows, cols] = part
        else:
            cs[slot, :, cols] = part.astype(BF16)

    def crossed(u):
        for n in range(2):
            cols = slice(n * 256, (n + 1) * 256)
            acc[:, cols] = jnp.dot(rr[rows_of(u, 256), :], xb[:, cols], preferred_element_type=F32)

    def back():
        @pl.loop(0, 8)
        def _(ap):
            for jp in range(4):
                cols = slice(jp * 128, (jp + 1) * 128)
                for ih in range(2):
                    v0 = acc[rows_of(ap * 4 + ih, 8), cols]
                    v1 = acc[rows_of(ap * 4 + 2 + ih, 8), cols]
                    turned = pltpu.roll(jnp.where(low8, v1, v0), 64, 1)
                    dd[ap, pl.ds(ih * 64 + 2 * jp, 8, stride=8), :] = jnp.where(low8, v0, turned)
                    dd[ap, pl.ds(ih * 64 + 2 * jp + 1, 8, stride=8), :] = jnp.where(low8, turned, v1)

    own_out = both(edge, origin)

    def give_back(n, u):
        crossed(u)
        back()
        for k in range(4):
            for ap in range(8):
                xs[n, k, :, ap * 128:(ap + 1) * 128] = dd[ap, k * 32:(k + 1) * 32, :].astype(BF16)
            put(xs.at[n, k], xr.at[v], s_o.at[n], r_o.at[v], device(yl, 2 * c + u, k // 2, z, k % 2),
                own=both(own_out, mu == u, q == k))

    u0 = jnp.where(origin, mu, 1 - mu)
    u1 = 1 - u0

    def prepare(u):
        apply_mask(u)
        reorder(u)

    @pl.when(origin)
    def _():
        rest_of_amplitudes(u0)
        prepare(u0)

    for near in (yh, 1 - yh):
        for p in range(LP):
            for u in range(2):
                dist = lax.rem(x - (2 * c + u) + 4, 4)
                for d in range(2):
                    passing = dist == (1, 3)[d]
                    k = near * 2 + d
                    arrived(mslot(u, k, p), r_m.at[u, k, p], cond=passing)
                    put(mslot(u, k, p), mslot(u, k, p), s_mf, r_m.at[u, k, p],
                        device(yh, xn[d], yl, z, c), cond=passing)

    for i in range(3):
        u, core = lax.rem(xsrc[i], 2), lax.div(xsrc[i], 2)
        arrived(tt.at[i], r_tt.at[i], cond=edge)
        put(tt.at[i], mslot(u, kt, LP), s_y.at[2, i], r_m.at[u, kt, LP], device(yh, x, 1 - yh, z, core),
            cond=edge)

    pass_ladder()
    for b in range(2):
        k = (b * 4 + zo) * 2 + c
        arrived(xslot(k), r_x.at[k])
        share_crossed(k)

    @pl.when(jnp.logical_not(origin))
    def _():
        rest_of_amplitudes(u0)
        prepare(u0)

    arrived(xslot(o), r_x.at[o])
    for b in range(2):
        for tz in range(4):
            k = (b * 4 + tz) * 2 + 1 - c
            arrived(xslot(k), r_x.at[k])
    give_back(0, u0)
    rest_of_amplitudes(u1)
    prepare(u1)
    rest_of_ladder(e0)

    def ccol(ref, k, j):
        return ref.at[k, :, pl.ds(j * 256, 256)]

    def to_core(j, k):
        put(ccol(cs, k, j), ccol(cr, k, j), s_c.at[k], r_c.at[k, j], device(yh, x, yl, z, 1 - c))

    def to_chip(j):
        arrived(ccol(cr, 0, j), r_c.at[0, j])
        cols = slice(j * 256, (j + 1) * 256)
        part = pp[rows_of((1 - yl) * 2 + c, 256), cols] + cr[0, :, cols].astype(F32)
        cs[2, :, cols] = part.astype(BF16)
        put(ccol(cs, 2, j), ccol(cr, 2, j), s_c.at[2], r_c.at[2, j], device(yh, x, 1 - yl, z, c))

    def ladder_chunk(j):
        far_ladder(j)
        ladder_second(e1, j, (1 - yl) * 2 + 1 - c, 0)
        to_core(j, 0)
        ladder_second(e1, j, yl * 2 + 1 - c, 1)
        to_core(j, 1)
        ladder_second(e1, j, (1 - yl) * 2 + c, None)
        ladder_second(e1, j, q, None)

    ladder_first(e0, 0)
    ladder_first(e0, 1)
    rest_of_ladder(e1)
    ladder_chunk(0)
    ladder_first(e0, 2)
    to_chip(0)
    ladder_chunk(1)
    ladder_first(e0, 3)
    to_chip(1)
    ladder_chunk(2)
    to_chip(2)
    give_back(1, u1)
    ladder_chunk(3)
    to_chip(3)

    act_out = jnp.logical_and(slot_a + 16 * x < cnt[2 * yh], slot_b < cnt[2 * yh + 1])
    mask_out = jnp.where(act_out, 1.0, 0.0).astype(F32)

    for d in range(3):
        arrived(lad, s_l.at[d], cond=None if d < 2 else c != ls)
    arrived(lb.at[pl.ds(0, 512)], s_lf)
    arrived(amp, s_m.at[0], cond=jnp.logical_not(own_out))
    arrived(amp, s_m.at[1])
    arrived(tb, s_mt, cond=edge)
    for d in range(2):
        arrived(mb.at[0, pl.ds(0, 4 * PR * LP)], s_mx.at[d], cond=origin)
        arrived(xt.at[d], s_t.at[d])
    arrived(mb.at[0, pl.ds(0, 2 * PR * LP)], s_mf)
    arrived(xt.at[2], s_tf)
    for i in range(3):
        arrived(xt.at[i], s_y.at[0, i], cond=jnp.logical_not(both(edge, c == lax.div(xsrc[i], 2))))
        arrived(xt.at[i], s_y.at[1, i])
        arrived(tt.at[i], s_y.at[2, i], cond=edge)
    arrived(xb.at[pl.ds(0, 256)], s_xa)
    arrived(xb.at[pl.ds(0, 2048)], s_xd)
    arrived(xb.at[pl.ds(0, 512)], s_xf)
    for d in range(2):
        arrived(xb.at[pl.ds(0, 512)], s_xz.at[d])
    for j in range(4):
        arrived(ccol(cr, 1, j), r_c.at[1, j])
        arrived(ccol(cr, 2, j), r_c.at[2, j])
    for k in range(3):
        arrived(cs.at[k], s_c.at[k])

    for kk in range(4):
        for k in (2 * kk, 2 * kk + 1):
            arrived(xr.at[k], r_o.at[k])
        got = [xr[k].astype(F32) for k in (2 * kk, 2 * kk + 1)]
        for i in range(4):
            at = i * 64 + kk * 16
            part = jnp.concatenate([g[i * 8:i * 8 + 8] for g in got], axis=0)
            part += cr[1, at:at + 16, :].astype(F32) + cr[2, at:at + 16, :].astype(F32)
            out[at:at + 16, :] = ((pp[rows_of(q * 16 + i * 4 + kk, 16), :] + part) * mask_out).astype(BF16)

    arrived(xs.at[0], s_o.at[0], cond=jnp.logical_not(own_out))
    arrived(xs.at[0, pl.ds(0, 3)], s_o.at[0], cond=own_out)
    arrived(xs.at[1], s_o.at[1])


def per_device(amplitudes, ladder_integrals, crossed_integrals, vir_counts):
    dma = pltpu.SemaphoreType.DMA
    hbm = pl.BlockSpec(memory_space=pl.ANY)
    return pl.pallas_call(
        kernel,
        out_shape=pltpu.VMEM((256, 1024), BF16),
        in_specs=[pl.BlockSpec(memory_space=pltpu.SMEM), hbm, hbm, hbm],
        out_specs=pl.BlockSpec(memory_space=pltpu.VMEM),
        scratch_shapes=[
            pltpu.VMEM((2, 1024, 1024), BF16),
            pltpu.VMEM((2048, 1024), BF16),
            pltpu.VMEM((4096, 512), BF16),
            pltpu.VMEM((256, 1024), BF16),
            pltpu.VMEM((3, 256 // NP, 1024), BF16),
            pltpu.VMEM((3, 256 // NP, 1024), BF16),
            pltpu.VMEM((2, 1024, 1024), BF16),
            pltpu.VMEM((1024, 1024), F32),
            pltpu.VMEM((512, 4096), BF16),
            pltpu.VMEM((1152, 128), F32),
            pltpu.VMEM((256, 512), F32),
            pltpu.VMEM((8, 128, 128), F32),
            pltpu.VMEM((3, 256, 1024), BF16),
            pltpu.VMEM((3, 256, 1024), BF16),
            pltpu.VMEM((2, 4, 32, 1024), BF16),
            pltpu.VMEM((8, 32, 1024), BF16),
            dma((3,)), dma, dma((2,)), dma, dma((2,)), dma, dma((2,)), dma, dma((3, 3)),
            dma, dma, dma((2,)), dma, dma((3,)), dma((2,)),
            dma((2, 4, NP)), dma((NP,)), dma((3,)), dma((3,)), dma((4, 2)), dma((4, 2, 4)), dma((16,)), dma((3, 4)), dma((8,)),
        ],
        compiler_params=pltpu.CompilerParams(
            collective_id=0, has_side_effects=True, vmem_limit_bytes=56 * 1024 * 1024
        ),
        name="residual",
    )(vir_counts, amplitudes, ladder_integrals, crossed_integrals)


def solution(mesh):
    in_specs = (P("occ", "vir"), P("occ", "vir"), P(None, "occ", "vir"), P())
    return jax.shard_map(
        per_device, mesh=mesh, in_specs=in_specs, out_specs=P("occ", "vir"), check_vma=False
    )
```

```python
import jax
import jax.numpy as jnp
from jax import lax
from jax.experimental import pallas as pl
from jax.experimental.pallas import tpu as pltpu
from jax.sharding import PartitionSpec as P

MESH = pl.DeviceIdType.MESH
F32 = jnp.float32
BF16 = jnp.bfloat16
NP = 4


def both(*conds):
    out = conds[0]
    for other in conds[1:]:
        out = jnp.logical_and(out, other)
    return out


def device(yh, x, yl, z, c):
    return (yh * 4 + x, (yl * 4 + z) * 2 + c)


def rows_of(k, size):
    return pl.ds(pl.multiple_of(k * size, size), size)


def kernel(
    cnt, amp, lad, xin, out,
    mb, lb, xb, tb, xt, tt, mm, pp, rr, ff, acc, dd, cs, cr, xs, xr,
    s_l, s_lf, s_m, s_mt, s_mx, s_mf, s_t, s_tf, s_y, s_xa, s_xd, s_xz, s_xf, s_c, s_o,
    r_m, r_t, r_xt, r_tt, r_l, r_lf, r_x, r_c, r_o,
):
    v = lax.axis_index("vir")
    o = lax.axis_index("occ")
    yh = lax.div(v, 4)
    x = lax.rem(v, 4)
    yl = lax.div(o, 8)
    z = lax.rem(lax.div(o, 2), 4)
    c = lax.rem(o, 2)
    xn = (lax.rem(x + 1, 4), lax.rem(x + 3, 4))
    zn = (lax.rem(z + 1, 4), lax.rem(z + 3, 4))
    zo = lax.rem(z + 2, 4)
    q = yl * 2 + c
    edge = yh == yl
    inner = jnp.logical_not(edge)

    def put(src, dst, ss, rs, target, cond=None, own=None):
        def go():
            pltpu.make_async_remote_copy(
                src_ref=src, dst_ref=dst, send_sem=ss, recv_sem=rs, device_id=target, device_id_type=MESH
            ).start()

        if own is not None:
            @pl.when(own)
            def _():
                pltpu.make_async_copy(src, dst, rs).start()

            cond = jnp.logical_not(own)
        if cond is None:
            go()
        else:
            pl.when(cond)(go)

    def arrived(ref, sem, cond=None):
        def go():
            pltpu.make_async_copy(ref, ref, sem).wait()

        if cond is None:
            go()
        else:
            pl.when(cond)(go)

    PR = 256 // NP

    def mslot(u, k, p):
        return mb.at[u, rows_of(k * NP + p, PR)]

    def lslot(t, hf):
        return lb.at[rows_of(t * 2 + hf, 256)]

    def xslot(k):
        return xb.at[rows_of(k, 256)]

    barrier = pltpu.get_barrier_semaphore()
    y = yh * 2 + yl
    peers = [device(yh, x, yl, z, 1 - c)]
    for tc in range(2):
        for d in range(2):
            ty = lax.rem(y + 1 + 2 * d, 4)
            peers.append(device(yh, xn[d], yl, z, tc))
            peers.append(device(lax.div(ty, 2), x, lax.rem(ty, 2), z, tc))
            peers.append(device(yh, x, yl, zn[d], tc))
    for peer in peers:
        pl.semaphore_signal(barrier, inc=1, device_id=peer, device_id_type=MESH)
    pl.semaphore_wait(barrier, len(peers))

    put(xin.at[1 - yl], xslot(o), s_xa, r_x.at[o], device(yh, x, 1 - yl, z, c))
    for d in range(2):
        put(xin.at[yl], xslot(o), s_xz.at[d], r_x.at[o], device(yh, x, yl, zn[d], c))
    ms = lax.div(x, 2)
    mu = lax.rem(x, 2)
    LP = NP - 1
    for d in range(2):
        put(amp.at[pl.ds(LP * PR, PR)], xt.at[d], s_t.at[d], r_xt.at[d], device(yh, xn[d], yl, z, c))
    for p in range(NP):
        part = amp.at[pl.ds(p * PR, PR)]
        put(part, mslot(mu, q, p), s_m.at[0], r_m.at[mu, q, p], device(yh, x, yh, z, ms),
            own=both(edge, c == ms))
        put(part, tb.at[pl.ds(p * PR, PR)], s_m.at[1], r_t.at[p], device(1 - yh, x, 1 - yl, z, c),
            cond=edge)
        put(part, mslot(mu, q, p), s_m.at[1], r_m.at[mu, q, p], device(1 - yh, x, yh, z, ms),
            cond=inner)
    pltpu.make_async_copy(xin.at[yl], xslot(o), r_x.at[o]).start()

    def share_crossed(k, src=None):
        put(xslot(k) if src is None else src, xslot(k), s_xd, r_x.at[k], device(yh, x, yl, z, 1 - c))

    share_crossed(o, xin.at[yl])
    ls = lax.div(z, 2)
    lt = 2 * lax.rem(z, 2) + c
    for hf in range(2):
        put(lad.at[pl.ds(hf * 256, 256)], lslot(lt, hf), s_l.at[2], r_l.at[lt, hf],
            device(yh, x, yl, z, ls), own=c == ls)

    op = ((1 - yl) * 4 + z) * 2 + c
    arrived(xslot(op), r_x.at[op])
    for d in range(2):
        put(xslot(op), xslot(op), s_xz.at[d], r_x.at[op], device(yh, x, yl, zn[d], c))

    def send_ladder(part):
        for d in range(2):
            hf = d if part == 0 else 1 - d
            put(lad.at[pl.ds(hf * 256, 256)], lslot(lt, hf), s_l.at[d], r_l.at[lt, hf],
                device(yh, x, yl, zn[d], ls))

    send_ladder(0)
    share_crossed(op)

    xsrc = (xn[1], xn[0], lax.rem(x + 2, 4))

    def along_y(i):
        xs_, part = xsrc[i], xt.at[i]
        arrived(part, r_xt.at[i])
        u, core = lax.rem(xs_, 2), lax.div(xs_, 2)
        put(part, mslot(u, q, LP), s_y.at[0, i], r_m.at[u, q, LP], device(yh, x, yh, z, core),
            own=both(edge, c == core))
        put(part, tt.at[i], s_y.at[1, i], r_tt.at[i], device(1 - yh, x, 1 - yl, z, c), cond=edge)
        put(part, mslot(u, q, LP), s_y.at[1, i], r_m.at[u, q, LP], device(1 - yh, x, yh, z, core),
            cond=inner)

    for i in range(2):
        along_y(i)
        put(xt.at[i], xt.at[2], s_tf, r_xt.at[2], device(yh, xn[i], yl, z, c), cond=c == i)

    origin = c == ms

    def spread_amplitudes(k, p):
        arrived(mslot(mu, k, p), r_m.at[mu, k, p], cond=origin)
        for d in range(2):
            put(mslot(mu, k, p), mslot(mu, k, p), s_mx.at[d], r_m.at[mu, k, p],
                device(yh, xn[d], yl, z, c), cond=origin)

    for p in range(LP):
        for e in range(2):
            spread_amplitudes(yh * 2 + e, p)

    def pass_crossed(b):
        k = (b * 4 + lax.rem(z + 3 + 2 * b, 4)) * 2 + c
        arrived(xslot(k), r_x.at[k])
        put(xslot(k), xslot(k), s_xf, r_x.at[k], device(yh, x, yl, lax.rem(z + 1 + 2 * b, 4), c))
        share_crossed(k)

    pass_crossed(yl)
    pass_crossed(1 - yl)
    send_ladder(1)
    for d in range(2):
        k = ((1 - d) * 4 + zn[1 - d]) * 2 + c
        arrived(xslot(k), r_x.at[k])
        share_crossed(k)

    along_y(2)

    kt = (1 - yl) * 2 + c
    for p in range(NP):
        part = tb.at[pl.ds(p * PR, PR)]
        arrived(part, r_t.at[p], cond=edge)
        put(part, mslot(mu, kt, p), s_mt, r_m.at[mu, kt, p], device(yh, x, 1 - yh, z, ms), cond=edge)
        if p < LP:
            for e in range(2):
                spread_amplitudes((1 - yh) * 2 + e, p)

    lane = lax.broadcasted_iota(jnp.int32, (1, 1024), 1)
    slot_a = lax.div(lane, 64)
    slot_b = lax.rem(lane, 64)
    low = lax.broadcasted_iota(jnp.int32, (16, 128), 1) < 64
    low8 = lax.broadcasted_iota(jnp.int32, (8, 128), 1) < 64

    def rest_of_amplitudes(u):
        dist = lax.rem(x - (2 * c + u) + 4, 4)
        for k in range(4):
            done = jnp.logical_or(dist == 0, dist == (1, 3)[k % 2])
            for p in range(LP):
                arrived(mslot(u, k, p), r_m.at[u, k, p], cond=jnp.logical_not(done))
            arrived(mslot(u, k, LP), r_m.at[u, k, LP])

    ldist = [lax.rem(z - (2 * c + u) + 4, 4) for u in range(2)]
    e1 = jnp.where(ldist[0] == 2, 0, 1)
    e0 = 1 - e1

    def rest_of_ladder(e):
        dist = lax.rem(z - (2 * c + e) + 4, 4)
        for hf in range(2):
            for t in range(2):
                arrived(lslot(2 * e + t, hf), r_l.at[2 * e + t, hf],
                        cond=both(dist != (1, 3)[hf], dist != 2))

    def lchunk(t, hf, j):
        return lb.at[rows_of(t * 2 + hf, 256), pl.ds(j * 256, 256)]

    def far_ladder(j):
        for hf in range(2):
            for t in range(2):
                arrived(lchunk(2 * e1 + t, hf, j), r_lf.at[2 * e1 + t, hf, j],
                        cond=lax.rem(z - (2 * c + e1) + 4, 4) == 2)

    def pass_ladder():
        for u in range(2):
            for d in range(2):
                for t in (2 * u, 2 * u + 1):
                    arrived(lslot(t, d), r_l.at[t, d], cond=ldist[u] == (1, 3)[d])
        for j in range(4):
            for u in range(2):
                for d in range(2):
                    for t in (2 * u, 2 * u + 1):
                        put(lchunk(t, d, j), lchunk(t, d, j), s_lf, r_lf.at[t, d, j],
                            device(yh, x, yl, zn[d], c), cond=ldist[u] == (1, 3)[d])

    def apply_mask(u):
        act = jnp.logical_and(slot_a + (32 * c + 16 * u) < cnt[2 * yl], slot_b < cnt[2 * yl + 1])
        mask = jnp.where(act, 1.0, 0.0).astype(BF16)

        @pl.loop(0, 32)
        def _(r):
            mm[u, rows_of(r, 32), :] = mb[u, rows_of(r, 32), :] * mask

    def reorder(u):
        @pl.loop(0, 8)
        def _(ap):
            @pl.loop(0, 16)
            def _(r):
                ff[pl.ds(pl.multiple_of(r * 72, 8), 64), :] = mm[u, rows_of(r, 64), rows_of(ap, 128)].astype(F32)

            for kp in range(32):
                v0 = ff[pl.ds(2 * kp, 16, stride=72), :]
                v1 = ff[pl.ds(2 * kp + 1, 16, stride=72), :]
                turned = pltpu.roll(jnp.where(low, v1, v0), 64, 1)
                pair = jnp.concatenate([jnp.where(low, v0, turned), jnp.where(low, turned, v1)], axis=0)
                rr[rows_of(u * 8 + ap, 32), kp * 128:(kp + 1) * 128] = pair.astype(BF16)

    def ladder_first(u, j):
        @pl.loop(0, 4)
        def _(t):
            rows, cols = rows_of(t, 256), slice(j * 256, (j + 1) * 256)
            pp[rows, cols] = jnp.dot(mm[u, rows, :], lb[rows_of(u, 1024), cols], preferred_element_type=F32)

    def ladder_second(u, j, b, slot):
        rows, cols = rows_of(b, 256), slice(j * 256, (j + 1) * 256)
        part = pp[rows, cols] + jnp.dot(mm[u, rows, :], lb[rows_of(u, 1024), cols], preferred_element_type=F32)
        if slot is None:
            pp[rows, cols] = part
        else:
            cs[slot, :, cols] = part.astype(BF16)

    def crossed(u):
        for n in range(2):
            cols = slice(n * 256, (n + 1) * 256)
            acc[:, cols] = jnp.dot(rr[rows_of(u, 256), :], xb[:, cols], preferred_element_type=F32)

    def back():
        @pl.loop(0, 8)
        def _(ap):
            for jp in range(4):
                cols = slice(jp * 128, (jp + 1) * 128)
                for ih in range(2):
                    v0 = acc[rows_of(ap * 4 + ih, 8), cols]
                    v1 = acc[rows_of(ap * 4 + 2 + ih, 8), cols]
                    turned = pltpu.roll(jnp.where(low8, v1, v0), 64, 1)
                    dd[ap, pl.ds(ih * 64 + 2 * jp, 8, stride=8), :] = jnp.where(low8, v0, turned)
                    dd[ap, pl.ds(ih * 64 + 2 * jp + 1, 8, stride=8), :] = jnp.where(low8, turned, v1)

    own_out = both(edge, origin)

    def give_back(n, u):
        crossed(u)
        back()
        for k in range(4):
            for ap in range(8):
                xs[n, k, :, ap * 128:(ap + 1) * 128] = dd[ap, k * 32:(k + 1) * 32, :].astype(BF16)
            put(xs.at[n, k], xr.at[v], s_o.at[n], r_o.at[v], device(yl, 2 * c + u, k // 2, z, k % 2),
                own=both(own_out, mu == u, q == k))

    u0 = jnp.where(origin, mu, 1 - mu)
    u1 = 1 - u0

    def prepare(u):
        apply_mask(u)
        reorder(u)

    @pl.when(origin)
    def _():
        rest_of_amplitudes(u0)
        prepare(u0)

    for near in (yh, 1 - yh):
        for p in range(LP):
            for u in range(2):
                dist = lax.rem(x - (2 * c + u) + 4, 4)
                for d in range(2):
                    passing = dist == (1, 3)[d]
                    k = near * 2 + d
                    arrived(mslot(u, k, p), r_m.at[u, k, p], cond=passing)
                    put(mslot(u, k, p), mslot(u, k, p), s_mf, r_m.at[u, k, p],
                        device(yh, xn[d], yl, z, c), cond=passing)

    for i in range(3):
        u, core = lax.rem(xsrc[i], 2), lax.div(xsrc[i], 2)
        arrived(tt.at[i], r_tt.at[i], cond=edge)
        put(tt.at[i], mslot(u, kt, LP), s_y.at[2, i], r_m.at[u, kt, LP], device(yh, x, 1 - yh, z, core),
            cond=edge)

    pass_ladder()
    for b in range(2):
        k = (b * 4 + zo) * 2 + c
        arrived(xslot(k), r_x.at[k])
        share_crossed(k)

    @pl.when(jnp.logical_not(origin))
    def _():
        rest_of_amplitudes(u0)
        prepare(u0)

    arrived(xslot(o), r_x.at[o])
    for b in range(2):
        for tz in range(4):
            k = (b * 4 + tz) * 2 + 1 - c
            arrived(xslot(k), r_x.at[k])
    give_back(0, u0)
    rest_of_amplitudes(u1)
    prepare(u1)
    give_back(1, u1)
    rest_of_ladder(e0)

    def ccol(ref, k, j):
        return ref.at[k, :, pl.ds(j * 256, 256)]

    def to_core(j, k):
        put(ccol(cs, k, j), ccol(cr, k, j), s_c.at[k], r_c.at[k, j], device(yh, x, yl, z, 1 - c))

    def to_chip(j):
        arrived(ccol(cr, 0, j), r_c.at[0, j])
        cols = slice(j * 256, (j + 1) * 256)
        part = pp[rows_of((1 - yl) * 2 + c, 256), cols] + cr[0, :, cols].astype(F32)
        cs[2, :, cols] = part.astype(BF16)
        put(ccol(cs, 2, j), ccol(cr, 2, j), s_c.at[2], r_c.at[2, j], device(yh, x, 1 - yl, z, c))

    def ladder_chunk(j):
        far_ladder(j)
        ladder_second(e1, j, (1 - yl) * 2 + 1 - c, 0)
        to_core(j, 0)
        ladder_second(e1, j, yl * 2 + 1 - c, 1)
        to_core(j, 1)
        ladder_second(e1, j, (1 - yl) * 2 + c, None)
        ladder_second(e1, j, q, None)

    ladder_first(e0, 0)
    ladder_first(e0, 1)
    rest_of_ladder(e1)
    ladder_chunk(0)
    ladder_first(e0, 2)
    to_chip(0)
    ladder_chunk(1)
    ladder_first(e0, 3)
    to_chip(1)
    ladder_chunk(2)
    to_chip(2)
    ladder_chunk(3)
    to_chip(3)

    act_out = jnp.logical_and(slot_a + 16 * x < cnt[2 * yh], slot_b < cnt[2 * yh + 1])
    mask_out = jnp.where(act_out, 1.0, 0.0).astype(F32)

    for d in range(3):
        arrived(lad, s_l.at[d], cond=None if d < 2 else c != ls)
    arrived(lb.at[pl.ds(0, 512)], s_lf)
    arrived(amp, s_m.at[0], cond=jnp.logical_not(own_out))
    arrived(amp, s_m.at[1])
    arrived(tb, s_mt, cond=edge)
    for d in range(2):
        arrived(mb.at[0, pl.ds(0, 4 * PR * LP)], s_mx.at[d], cond=origin)
        arrived(xt.at[d], s_t.at[d])
    arrived(mb.at[0, pl.ds(0, 2 * PR * LP)], s_mf)
    arrived(xt.at[2], s_tf)
    for i in range(3):
        arrived(xt.at[i], s_y.at[0, i], cond=jnp.logical_not(both(edge, c == lax.div(xsrc[i], 2))))
        arrived(xt.at[i], s_y.at[1, i])
        arrived(tt.at[i], s_y.at[2, i], cond=edge)
    arrived(xb.at[pl.ds(0, 256)], s_xa)
    arrived(xb.at[pl.ds(0, 2048)], s_xd)
    arrived(xb.at[pl.ds(0, 512)], s_xf)
    for d in range(2):
        arrived(xb.at[pl.ds(0, 512)], s_xz.at[d])
    for j in range(4):
        arrived(ccol(cr, 1, j), r_c.at[1, j])
        arrived(ccol(cr, 2, j), r_c.at[2, j])
    for k in range(3):
        arrived(cs.at[k], s_c.at[k])

    for kk in range(4):
        for k in (2 * kk, 2 * kk + 1):
            arrived(xr.at[k], r_o.at[k])
        got = [xr[k].astype(F32) for k in (2 * kk, 2 * kk + 1)]
        for i in range(4):
            at = i * 64 + kk * 16
            part = jnp.concatenate([g[i * 8:i * 8 + 8] for g in got], axis=0)
            part += cr[1, at:at + 16, :].astype(F32) + cr[2, at:at + 16, :].astype(F32)
            out[at:at + 16, :] = ((pp[rows_of(q * 16 + i * 4 + kk, 16), :] + part) * mask_out).astype(BF16)

    arrived(xs.at[0], s_o.at[0], cond=jnp.logical_not(own_out))
    arrived(xs.at[0, pl.ds(0, 3)], s_o.at[0], cond=own_out)
    arrived(xs.at[1], s_o.at[1])


def per_device(amplitudes, ladder_integrals, crossed_integrals, vir_counts):
    dma = pltpu.SemaphoreType.DMA
    hbm = pl.BlockSpec(memory_space=pl.ANY)
    return pl.pallas_call(
        kernel,
        out_shape=pltpu.VMEM((256, 1024), BF16),
        in_specs=[pl.BlockSpec(memory_space=pltpu.SMEM), hbm, hbm, hbm],
        out_specs=pl.BlockSpec(memory_space=pltpu.VMEM),
        scratch_shapes=[
            pltpu.VMEM((2, 1024, 1024), BF16),
            pltpu.VMEM((2048, 1024), BF16),
            pltpu.VMEM((4096, 512), BF16),
            pltpu.VMEM((256, 1024), BF16),
            pltpu.VMEM((3, 256 // NP, 1024), BF16),
            pltpu.VMEM((3, 256 // NP, 1024), BF16),
            pltpu.VMEM((2, 1024, 1024), BF16),
            pltpu.VMEM((1024, 1024), F32),
            pltpu.VMEM((512, 4096), BF16),
            pltpu.VMEM((1152, 128), F32),
            pltpu.VMEM((256, 512), F32),
            pltpu.VMEM((8, 128, 128), F32),
            pltpu.VMEM((3, 256, 1024), BF16),
            pltpu.VMEM((3, 256, 1024), BF16),
            pltpu.VMEM((2, 4, 32, 1024), BF16),
            pltpu.VMEM((8, 32, 1024), BF16),
            dma((3,)), dma, dma((2,)), dma, dma((2,)), dma, dma((2,)), dma, dma((3, 3)),
            dma, dma, dma((2,)), dma, dma((3,)), dma((2,)),
            dma((2, 4, NP)), dma((NP,)), dma((3,)), dma((3,)), dma((4, 2)), dma((4, 2, 4)), dma((16,)), dma((3, 4)), dma((8,)),
        ],
        compiler_params=pltpu.CompilerParams(
            collective_id=0, has_side_effects=True, vmem_limit_bytes=56 * 1024 * 1024
        ),
        name="residual",
    )(vir_counts, amplitudes, ladder_integrals, crossed_integrals)


def solution(mesh):
    in_specs = (P("occ", "vir"), P("occ", "vir"), P(None, "occ", "vir"), P())
    return jax.shard_map(
        per_device, mesh=mesh, in_specs=in_specs, out_specs=P("occ", "vir"), check_vma=False
    )
```
